32 devices in a mesh: fsdp: 16 (over z, y, x), rep: 2 (over core).
Axes of the slice: x: 2, y: 2, z: 4, core: 2. Of those that a mesh axis runs over, the one named last changes fastest.
Arguments:
- queries: bfloat16 [8192, 2048], P(('fsdp', 'rep')), may hold values from -6 to 6
- key_rows: bfloat16 [8192, 2048], P(('fsdp', 'rep')), may hold values from -6 to 6
- values: bfloat16 [8192, 2048], P(('fsdp', 'rep')), may hold values from -6 to 6
- cotangent: bfloat16 [8192, 2048], P(('fsdp', 'rep')), may hold values from -6 to 6
- out_weight: bfloat16 [2048, 2048], P('fsdp'), may hold values from -0.125 to 0.125
- prob_bits: int32 [2, 8192, 1024], P(None, ('fsdp', 'rep')), may hold values from 0 to 255
- out_bits: int32 [2, 8192, 256], P(None, ('fsdp', 'rep')), may hold values from 0 to 255
Outputs:
- query_grad: bfloat16 [8192, 2048], P(('fsdp', 'rep'))
- key_grad: bfloat16 [8192, 2048], P(('fsdp', 'rep'))
- value_grad: bfloat16 [8192, 2048], P(('fsdp', 'rep'))
- weight_grad: float32 [2048, 2048], P('fsdp')
The draws below stay inside these ranges and needn't reach their ends.
All inputs are finite; a program needn't handle non-finite values.
Results may differ from the reference program's by a relative error of at most 0.019.
Values may be sent and summed in bfloat16 or wider, within the bound.
No kernel may reach another device: no remote copies, remote signals or barrier semaphores. Data moves between devices by JAX's collectives and lax.ppermute only.
A program may use at most 128 MiB of HBM per device.

```python
import jax
import jax.numpy as jnp
from jax import lax

HEADS = 32
HD = 64
DM = 2048
LENGTH = 256
INNER = 2048
SEQUENCES = 32
TOKENS = 8192


def drawn_pair(key):
    base = jax.random.fold_in(key, 101)
    seq_shape = (SEQUENCES, LENGTH, HEADS, HD)
    query_base = jnp.clip(jax.random.normal(jax.random.fold_in(base, 2), seq_shape), -6.0, 6.0)
    key_base = jnp.clip(jax.random.normal(jax.random.fold_in(base, 3), seq_shape), -6.0, 6.0)
    return (query_base.reshape(TOKENS, INNER), key_base.reshape(TOKENS, INNER))


def draw_queries(key, part):
    return drawn_pair(key)[0].astype(jnp.bfloat16)


def draw_key_rows(key, part):
    return drawn_pair(key)[1].astype(jnp.bfloat16)


def set_ends(array, key, least, largest):
    shape = array.shape
    place = [jax.random.randint(jax.random.fold_in(key, axis), (), 0, shape[axis]) for axis in range(len(shape))]
    array = array.at[tuple(place)].set(least)
    longest = shape.index(max(shape))
    place[longest] = (place[longest] + 1) % shape[longest]
    return array.at[tuple(place)].set(largest)


def level_of(own_key, shape, pieces, least, top_value):
    level, own = 1.0, jax.random.fold_in(own_key, 6)
    for position, shards_of in pieces:
        draws = jnp.exp(jax.random.uniform(jax.random.fold_in(own, position), (shards_of,), jnp.float32, least / len(pieces), top_value / len(pieces)))
        level = level * jnp.repeat(draws, shape[position] // shards_of).reshape([-1 if axis == position else 1 for axis in range(len(shape))])
    return level


def normal_values(key, shape, spread, reach, shards=(), held_as=jnp.bfloat16):
    result = spread * jax.random.normal(key, shape, jnp.float32)
    if shards:
        result = result * level_of(key, shape, shards, -0.22, 0.18)
    return jnp.clip(result, -reach, reach).astype(held_as)


def setup_inputs(seed: int = 0) -> dict:
    key_of = jax.random.split(jax.random.key(seed), 8)
    return {
        "queries": draw_queries(jax.random.fold_in(key_of[7], 71), 0),
        "key_rows": draw_key_rows(jax.random.fold_in(key_of[7], 71), 0),
        "values": normal_values(key_of[2], (TOKENS, INNER), 1.0, 6.0, ((0, 32),)),
        "cotangent": normal_values(key_of[3], (TOKENS, DM), 1.0, 6.0, ((0, 32),)),
        "out_weight": normal_values(key_of[4], (INNER, DM), INNER ** -0.5, 0.125, ((0, 16),)),
        "prob_bits": set_ends(jax.random.randint(key_of[5], (2, TOKENS, HEADS * LENGTH // 8), 0, 256), jax.random.fold_in(key_of[5], 1), 0, 255).astype(jnp.int32),
        "out_bits": set_ends(jax.random.randint(key_of[6], (2, TOKENS, DM // 8), 0, 256), jax.random.fold_in(key_of[6], 1), 0, 255).astype(jnp.int32),
    }


KEEP_SCALE = 4.0 / 3.0


def unpack_keep(bit_words):
    shifts = jnp.arange(8, dtype=jnp.int32)
    both_bits = bit_words[0] & bit_words[1]
    dropped_bit = jnp.right_shift(both_bits[..., None], shifts) & 1
    keep_mask = 1.0 - dropped_bit.astype(jnp.float32)
    return keep_mask.reshape(both_bits.shape[:-1] + (both_bits.shape[-1] * 8,))


def one_sequence(inputs):
    query_rows, key_block, value_rows, grad_rows, bit_words = inputs
    score_scale = HD ** -0.5
    query_rows = query_rows.astype(jnp.float32)
    key_block = key_block.astype(jnp.float32)
    value_rows = value_rows.astype(jnp.float32)
    grad_rows = grad_rows.astype(jnp.float32)
    keep_mask = unpack_keep(bit_words).reshape(LENGTH, HEADS, LENGTH)
    scores = jnp.einsum("qhd,khd->qhk", query_rows, key_block) * score_scale
    probabilities = jax.nn.softmax(scores, axis=-1)
    dropped = (probabilities * keep_mask * KEEP_SCALE).astype(jnp.bfloat16)
    dropped_wide = dropped.astype(jnp.float32)
    context = jnp.einsum("qhk,khd->qhd", dropped_wide, value_rows).astype(jnp.bfloat16)
    value_grad = jnp.einsum("qhk,qhd->khd", dropped_wide, grad_rows).astype(jnp.bfloat16)
    prob_grad = jnp.einsum("qhd,khd->qhk", grad_rows, value_rows) * keep_mask * KEEP_SCALE
    row_total = jnp.sum(prob_grad * probabilities, axis=-1, keepdims=True)
    score_grad = (probabilities * (prob_grad - row_total)).astype(jnp.bfloat16).astype(jnp.float32)
    query_grad = (jnp.einsum("qhk,khd->qhd", score_grad, key_block) * score_scale).astype(jnp.bfloat16)
    key_grad = (jnp.einsum("qhk,qhd->khd", score_grad, query_rows) * score_scale).astype(jnp.bfloat16)
    return context, query_grad, key_grad, value_grad


def reference(queries, key_rows, values, cotangent, out_weight, prob_bits, out_bits):
    keep_out = unpack_keep(out_bits)
    out_grad = (cotangent.astype(jnp.float32) * keep_out * KEEP_SCALE).astype(jnp.bfloat16)
    context_grad = jnp.dot(out_grad, out_weight.T, preferred_element_type=jnp.float32).astype(jnp.bfloat16)
    seq_shape = (SEQUENCES, LENGTH, HEADS, HD)
    word_blocks = jnp.swapaxes(prob_bits.reshape(2, SEQUENCES, LENGTH, HEADS * LENGTH // 8), 0, 1)
    context, query_grad, key_grad, value_grad = lax.map(
        one_sequence,
        (queries.reshape(seq_shape), key_rows.reshape(seq_shape), values.reshape(seq_shape),
         context_grad.reshape(seq_shape), word_blocks))
    context = context.reshape(TOKENS, INNER)
    weight_grad = jnp.dot(context.T, out_grad, preferred_element_type=jnp.float32) / SEQUENCES
    return (query_grad.reshape(TOKENS, INNER), key_grad.reshape(TOKENS, INNER),
            value_grad.reshape(TOKENS, INNER), weight_grad)
```

```python
import functools

import jax
import jax.numpy as jnp
from jax import lax
from jax.experimental import pallas as pl
from jax.experimental.pallas import tpu as pltpu
from jax.sharding import PartitionSpec as P

HD = 64
LENGTH = 256
BITS = 8
PLANE = 4
KEEP_SCALE = 4.0 / 3.0
SCORE_SCALE = HD ** (-0.5)
LOG2E = 1.4426950408889634
EXP_SCALE = SCORE_SCALE * LOG2E


def unpack_keep(bit_words):
    shifts = jnp.arange(BITS, dtype=jnp.int32)
    both_bits = bit_words[0] & bit_words[1]
    dropped_bit = jnp.right_shift(both_bits[..., None], shifts) & 1
    keep_mask = 1.0 - dropped_bit.astype(jnp.float32)
    return keep_mask.reshape(both_bits.shape[:-1] + (both_bits.shape[-1] * BITS,))


def one_sequence(inputs):
    query_rows, key_block, value_rows, grad_rows, bit_words = inputs
    head_count = query_rows.shape[1]
    keep_mask = unpack_keep(bit_words).reshape(LENGTH, head_count, LENGTH)
    scores = (
        jnp.einsum("qhd,khd->qhk", query_rows, key_block, preferred_element_type=jnp.float32)
        * SCORE_SCALE
    )
    probabilities = jax.nn.softmax(scores, axis=-1)
    dropped = (probabilities * keep_mask * KEEP_SCALE).astype(jnp.bfloat16)
    context = jnp.einsum(
        "qhk,khd->qhd", dropped, value_rows, preferred_element_type=jnp.float32
    ).astype(jnp.bfloat16)
    value_grad = jnp.einsum(
        "qhk,qhd->khd", dropped, grad_rows, preferred_element_type=jnp.float32
    ).astype(jnp.bfloat16)
    prob_grad = (
        jnp.einsum("qhd,khd->qhk", grad_rows, value_rows, preferred_element_type=jnp.float32)
        * keep_mask
        * KEEP_SCALE
    )
    row_total = jnp.sum(prob_grad * probabilities, axis=-1, keepdims=True)
    score_grad = (probabilities * (prob_grad - row_total)).astype(jnp.bfloat16)
    query_grad = (
        jnp.einsum("qhk,khd->qhd", score_grad, key_block, preferred_element_type=jnp.float32)
        * SCORE_SCALE
    ).astype(jnp.bfloat16)
    key_grad = (
        jnp.einsum("qhk,qhd->khd", score_grad, query_rows, preferred_element_type=jnp.float32)
        * SCORE_SCALE
    ).astype(jnp.bfloat16)
    return (context, query_grad, key_grad, value_grad)


def general(queries, key_rows, values, cotangent, out_weight, prob_bits, out_bits):
    tokens, inner_width = queries.shape
    seq_count = tokens // LENGTH
    head_count = inner_width // HD
    keep_out = unpack_keep(out_bits)
    out_grad = (cotangent.astype(jnp.float32) * keep_out * KEEP_SCALE).astype(jnp.bfloat16)
    context_grad = lax.dot_general(
        out_grad,
        lax.all_gather(out_weight, "fsdp", axis=0, tiled=True),
        (((1,), (1,)), ((), ())),
        preferred_element_type=jnp.float32,
    ).astype(jnp.bfloat16)
    seq_shape = (seq_count, LENGTH, head_count, HD)
    word_blocks = jnp.swapaxes(prob_bits.reshape(2, seq_count, LENGTH, prob_bits.shape[2]), 0, 1)
    context, query_grad, key_grad, value_grad = lax.map(
        one_sequence,
        (
            queries.reshape(seq_shape),
            key_rows.reshape(seq_shape),
            values.reshape(seq_shape),
            context_grad.reshape(seq_shape),
            word_blocks,
        ),
    )
    context = context.reshape(tokens, inner_width)
    sequences = float(seq_count * lax.axis_size("fsdp") * lax.axis_size("rep"))
    product = lax.dot_general(
        context, out_grad, (((0,), (0,)), ((), ())), preferred_element_type=jnp.float32
    )
    full_grad = product / sequences
    halves = lax.psum_scatter(
        full_grad.astype(jnp.bfloat16), "rep", scatter_dimension=1, tiled=True
    ).astype(jnp.float32)
    owned_half = lax.psum_scatter(halves, "fsdp", scatter_dimension=0, tiled=True)
    weight_grad = lax.all_gather(owned_half.astype(jnp.bfloat16), "rep", axis=1, tiled=True).astype(
        owned_half.dtype
    )
    return (
        query_grad.reshape(tokens, inner_width),
        key_grad.reshape(tokens, inner_width),
        value_grad.reshape(tokens, inner_width),
        weight_grad,
    )


def grad_kernel(cot_ref, bits_ref, out_ref):
    columns = cot_ref.shape[1]
    step = pl.program_id(0)
    words = bits_ref[0] & bits_ref[1]
    words = words.astype(jnp.float32).astype(jnp.bfloat16)
    count = words.shape[1]
    place = lax.broadcasted_iota(jnp.int32, (count, columns), 1)
    row = lax.broadcasted_iota(jnp.int32, (count, columns), 0)
    spread = (row == step * (columns // BITS) + place // BITS).astype(jnp.float32).astype(jnp.bfloat16)
    wide = jnp.dot(words, spread, preferred_element_type=jnp.float32).astype(jnp.int32)
    bit = jnp.left_shift(1, lax.broadcasted_iota(jnp.int32, wide.shape, 1) % BITS)
    scaled = cot_ref[...].astype(jnp.float32) * KEEP_SCALE
    out_ref[...] = jnp.where((wide & bit) == 0, scaled, 0.0).astype(out_ref.dtype)


def out_grad_of(cotangent, out_bits):
    tokens, width = cotangent.shape
    block = width // 4
    return pl.pallas_call(
        grad_kernel,
        grid=(width // block,),
        in_specs=[
            pl.BlockSpec((tokens, block), lambda i: (0, i)),
            pl.BlockSpec(out_bits.shape, lambda i: (0, 0, 0)),
        ],
        out_specs=pl.BlockSpec((tokens, block), lambda i: (0, i)),
        out_shape=jax.ShapeDtypeStruct(cotangent.shape, cotangent.dtype),
        name="outgrad",
    )(cotangent, out_bits)


def one_head(flat_t, head):
    rows = lax.broadcasted_iota(jnp.int32, flat_t.shape, 0) // HD
    return jnp.where(rows == head, flat_t, jnp.zeros_like(flat_t))


def dropped_bits(words_ref, first, count):
    rows = [words_ref[pl.ds(first + m, BITS, stride=0), :] for m in range(count)]
    wide = jnp.concatenate(rows, axis=0)
    bit = jnp.left_shift(1, lax.broadcasted_iota(jnp.int32, wide.shape, 0) % BITS)
    return wide & bit


def forward_kernel(owner_ref, q_ref, k_ref, v_ref, bits_ref, c0, c1, c2, c3, wt_ref, lse_ref, words_ref):
    step = pl.program_id(0)
    owner = owner_ref[step]
    words_ref[...] = (bits_ref[0] & bits_ref[1]).T
    half = words_ref.shape[0] // 2
    wt_ref[...] = words_ref[pl.ds(pl.multiple_of((owner % 2) * half, half), half), :]
    q_t = q_ref[...].T
    v_t = v_ref[...].T
    key_rows = k_ref[...]
    parts = []
    stats = []
    for head in range(2):
        s_t = jnp.dot(key_rows, one_head(q_t, head), preferred_element_type=jnp.float32)
        top = jnp.max(s_t, axis=0, keepdims=True)
        e_t = jnp.exp2((s_t - top) * EXP_SCALE)
        total = jnp.sum(e_t, axis=0, keepdims=True)
        stats.append(top * EXP_SCALE + jnp.log2(total))
        gone = dropped_bits(wt_ref, head * (half // 2), half // 2)
        dropped = jnp.where(gone == 0, e_t * (KEEP_SCALE / total), 0.0).astype(jnp.bfloat16)
        parts.append(
            jnp.dot(v_t[head * HD : (head + 1) * HD], dropped, preferred_element_type=jnp.float32)
        )
    lse_ref[0] = jnp.concatenate(stats * 4, axis=0)
    context_t = jnp.concatenate(parts, axis=0).astype(jnp.bfloat16)
    per = pl.num_programs(0) // PLANE
    for r, ref in enumerate((c0, c1, c2, c3)):

        @pl.when(step // per == r)
        def _(ref=ref):
            ref[...] = context_t


def forward(owners, queries, key_rows, values, prob_bits):
    tokens, width = queries.shape
    steps = width // (2 * HD)
    per = steps // PLANE
    words = prob_bits.shape[2] // steps
    block = pl.BlockSpec((tokens, 2 * HD), lambda i, o: (0, o[i]))

    def turn(r):
        return lambda i, o: (jnp.clip(i - r * per, 0, per - 1), 0)

    return pl.pallas_call(
        forward_kernel,
        grid_spec=pltpu.PrefetchScalarGridSpec(
            num_scalar_prefetch=1,
            grid=(steps,),
            in_specs=[
                block,
                block,
                block,
                pl.BlockSpec((2, tokens, 2 * words), lambda i, o: (0, 0, o[i] // 2)),
            ],
            out_specs=[pl.BlockSpec((2 * HD, tokens), turn(r)) for r in range(PLANE)]
            + [
                pl.BlockSpec((words, tokens), lambda i, o: (o[i], 0)),
                pl.BlockSpec((1, 8, tokens), lambda i, o: (o[i], 0, 0)),
            ],
            scratch_shapes=[pltpu.VMEM((2 * words, tokens), jnp.int32)],
        ),
        out_shape=[jax.ShapeDtypeStruct((per * 2 * HD, tokens), jnp.bfloat16)] * PLANE
        + [
            jax.ShapeDtypeStruct((steps * words, tokens), jnp.int32),
            jax.ShapeDtypeStruct((steps, 8, tokens), jnp.float32),
        ],
        name="forward",
    )(owners, queries, key_rows, values, prob_bits)


def backward_kernel(owner_ref, q_ref, k_ref, v_ref, wt_ref, lse_ref, g_ref, *rest):
    dq_ref, dk_ref, dv_ref = rest[-3:]
    q = q_ref[...]
    key_rows = k_ref[...]
    value_rows = v_ref[...]
    q_t = q.T
    k_t = key_rows.T
    g_t = g_ref[...]
    g = g_t.T
    half = wt_ref.shape[0]
    lanes = lax.broadcasted_iota(jnp.int32, q.shape, 1) // HD
    dq_t, dk, dv = [], None, None
    for head in range(2):
        s_t = jnp.dot(key_rows, one_head(q_t, head), preferred_element_type=jnp.float32)
        p_t = jnp.exp2(s_t * EXP_SCALE - lse_ref[0, head : head + 1, :])
        keep = dropped_bits(wt_ref, head * (half // 2), half // 2) == 0
        dropped = jnp.where(keep, p_t * KEEP_SCALE, 0.0).astype(jnp.bfloat16)
        raw_t = jnp.dot(value_rows, one_head(g_t, head), preferred_element_type=jnp.float32)
        grad_t = jnp.where(keep, raw_t * KEEP_SCALE, 0.0)
        total = jnp.sum(grad_t * p_t, axis=0, keepdims=True)
        ds_t = (p_t * (grad_t - total)).astype(jnp.bfloat16)
        dv_h = jnp.dot(dropped, g, preferred_element_type=jnp.float32)
        dk_h = jnp.dot(ds_t, q, preferred_element_type=jnp.float32)
        dq_t.append(
            jnp.dot(k_t[head * HD : (head + 1) * HD], ds_t, preferred_element_type=jnp.float32)
        )
        dv = dv_h if dv is None else jnp.where(lanes == head, dv_h, dv)
        dk = dk_h if dk is None else jnp.where(lanes == head, dk_h, dk)
    dq_ref[...] = (jnp.concatenate(dq_t, axis=0) * SCORE_SCALE).astype(dq_ref.dtype).T
    dk_ref[...] = (dk * SCORE_SCALE).astype(dk_ref.dtype)
    dv_ref[...] = dv.astype(dv_ref.dtype)


def backward(owners, queries, key_rows, values, words_t, lse, context_grad_t, into):
    tokens, width = queries.shape
    total = width // (2 * HD)
    steps = owners.shape[0]
    words = words_t.shape[0] // total
    block = pl.BlockSpec((tokens, 2 * HD), lambda i, o: (0, o[i]))
    whole = pl.BlockSpec(memory_space=pl.ANY)
    given = () if into is None else tuple(into)
    return pl.pallas_call(
        backward_kernel,
        grid_spec=pltpu.PrefetchScalarGridSpec(
            num_scalar_prefetch=1,
            grid=(steps,),
            in_specs=[
                block,
                block,
                block,
                pl.BlockSpec((words, tokens), lambda i, o: (o[i], 0)),
                pl.BlockSpec((1, 8, tokens), lambda i, o: (o[i], 0, 0)),
                pl.BlockSpec((2 * HD, tokens), lambda i, o: (i, 0)),
            ]
            + [whole] * len(given),
            out_specs=[block] * 3,
        ),
        out_shape=[jax.ShapeDtypeStruct(queries.shape, queries.dtype)] * 3,
        input_output_aliases={7 + n: n for n in range(len(given))},
        name="backward",
    )(owners, queries, key_rows, values, words_t, lse, context_grad_t, *given)


def collect_kernel(core_ref, own_ref, *rest):
    out_ref = rest[-1]
    halves = rest[:-1]
    rows = own_ref.shape[0]
    half = rows // 2
    core = core_ref[0]
    out_ref[0:rows, :] = own_ref[...]
    for n in range(len(halves) // 2):
        base = rows * (n + 1)
        mine = pl.multiple_of(base + core * half, half)
        theirs = pl.multiple_of(base + (1 - core) * half, half)
        out_ref[pl.ds(mine, half), :] = halves[2 * n][...]
        out_ref[pl.ds(theirs, half), :] = halves[2 * n + 1][...]


def collect(core, own, halves):
    rows, width = own.shape
    count = len(halves) // 2 + 1
    full = pl.BlockSpec(memory_space=pltpu.VMEM)
    return pl.pallas_call(
        collect_kernel,
        in_specs=[pl.BlockSpec(memory_space=pltpu.SMEM)] + [full] * (1 + len(halves)),
        out_specs=full,
        out_shape=jax.ShapeDtypeStruct((rows * count, width), own.dtype),
        name="collect",
    )(core, own, *halves)


def context_grad_kernel(w_ref, g_ref, out_ref):
    out_ref[...] = lax.dot_general(
        w_ref[...], g_ref[...], (((1,), (1,)), ((), ())), preferred_element_type=jnp.float32
    ).astype(out_ref.dtype)


def context_grad_of(weights, out_grad):
    full = pl.BlockSpec(memory_space=pltpu.VMEM)
    return pl.pallas_call(
        context_grad_kernel,
        in_specs=[full, full],
        out_specs=full,
        out_shape=jax.ShapeDtypeStruct((weights.shape[0], out_grad.shape[0]), jnp.bfloat16),
        name="contextgrad",
    )(weights, out_grad)


def weight_kernel(info_ref, c0, c1, c2, c3, g0, g1, g2, g3, keep_ref, send_ref, acc_ref):
    acc = None
    for c, g in ((c0, g0), (c1, g1), (c2, g2), (c3, g3)):
        part = jnp.dot(c[...], g[...], preferred_element_type=jnp.float32)
        acc = part if acc is None else acc + part
    acc_ref[...] = acc
    half = acc_ref.shape[0] // 2
    core = info_ref[0]
    keep_ref[0] = acc_ref[pl.ds(pl.multiple_of(core * half, half), half), :]
    send_ref[0] = acc_ref[pl.ds(pl.multiple_of((1 - core) * half, half), half), :].astype(
        send_ref.dtype
    )


def weight_partials(info, line, contexts_t, out_grads):
    tokens, width = out_grads[0].shape
    rows = contexts_t[0].shape[0] // line
    half = rows // 2
    context_spec = pl.BlockSpec((rows, tokens), lambda k, s: ((s[1] + k) % line, 0))
    grad_spec = pl.BlockSpec((tokens, width), lambda k, s: (0, 0))
    out_spec = pl.BlockSpec((1, half, width), lambda k, s: (k, 0, 0))
    return pl.pallas_call(
        weight_kernel,
        grid_spec=pltpu.PrefetchScalarGridSpec(
            num_scalar_prefetch=1,
            grid=(line,),
            in_specs=[context_spec] * PLANE + [grad_spec] * PLANE,
            out_specs=[out_spec, out_spec],
            scratch_shapes=[pltpu.VMEM((rows, width), jnp.float32)],
        ),
        out_shape=[
            jax.ShapeDtypeStruct((line, half, width), jnp.float32),
            jax.ShapeDtypeStruct((line, half, width), jnp.bfloat16),
        ],
        name="weightgrad",
    )(info, *contexts_t, *out_grads)


def pair_kernel(keep_ref, got_ref, own_ref, *sends):
    own_ref[...] = keep_ref[0] + got_ref[0].astype(jnp.float32)
    for k, ref in enumerate(sends):
        ref[...] = (keep_ref[k + 1] + got_ref[k + 1].astype(jnp.float32)).astype(ref.dtype)


def pair_sum(keep, got):
    line, half, width = keep.shape
    columns = width // 4
    spec = pl.BlockSpec((line, half, columns), lambda i: (0, 0, i))
    out = pl.BlockSpec((half, columns), lambda i: (0, i))
    return pl.pallas_call(
        pair_kernel,
        grid=(4,),
        in_specs=[spec, spec],
        out_specs=[out] * line,
        out_shape=[jax.ShapeDtypeStruct((half, width), jnp.float32)]
        + [jax.ShapeDtypeStruct((half, width), jnp.bfloat16)] * (line - 1),
        name="pairsum",
    )(keep, got)


def line_kernel(scale, own_ref, *rest):
    out_ref = rest[-1]
    total = own_ref[...]
    for ref in rest[:-1]:
        total = total + ref[...].astype(jnp.float32)
    out_ref[...] = total * scale


def line_sum(own, got, scale):
    full = pl.BlockSpec(memory_space=pltpu.VMEM)
    return pl.pallas_call(
        functools.partial(line_kernel, scale),
        in_specs=[full] * (1 + len(got)),
        out_specs=full,
        out_shape=jax.ShapeDtypeStruct(own.shape, jnp.float32),
        name="linesum",
    )(own, *got)


def planar(queries, key_rows, values, cotangent, out_weight, prob_bits, out_bits):
    chips = lax.axis_size("fsdp")
    line = chips // PLANE
    sequences = float(chips * lax.axis_size("rep"))
    core = lax.axis_index("rep").astype(jnp.int32)
    place = lax.axis_index("fsdp").astype(jnp.int32)
    z, p = place // PLANE, place % PLANE
    half = out_weight.shape[0] // 2

    def across(x, r):
        return lax.ppermute(x, "fsdp", [(f, f ^ r) for f in range(chips)])

    def along(x, k):
        return lax.ppermute(x, "fsdp", [(f, (f + PLANE * k) % chips) for f in range(chips)])

    def swap(x):
        return lax.ppermute(x, "rep", [(0, 1), (1, 0)])

    out_grad = out_grad_of(cotangent, out_bits)
    tokens = out_grad.shape[0]
    grad_x = across(out_grad, 1)
    grad_y = across(out_grad, 2)
    mine = lax.dynamic_slice_in_dim(out_weight, core * half, half, axis=0)
    halves = [along(mine, k) for k in range(1, line)]

    turns = jnp.arange(PLANE * line, dtype=jnp.int32)
    forward_owners = PLANE * (turns % line) + (p ^ (turns // line))
    *contexts_t, words_t, lse = forward(forward_owners, queries, key_rows, values, prob_bits)

    diag_top = across(grad_x[: tokens // 2], 2)
    diag_low = across(grad_y[tokens // 2 :], 1)

    pieces = []
    for h in halves:
        pieces += [h, swap(h)]
    weights = collect(core[None], out_weight, pieces)
    got_contexts = [contexts_t[0]] + [across(contexts_t[r], r) for r in range(1, PLANE)]
    grad_d = jnp.concatenate([diag_top, diag_low], axis=0)
    out_grads = [out_grad, grad_x, grad_y, grad_d]
    made = [context_grad_of(weights, g) for g in out_grads]
    context_grads = [made[0]] + [across(made[r], r) for r in range(1, PLANE)]

    info = jnp.stack([core, z])
    keep, send = weight_partials(info, line, got_contexts, out_grads)
    own, *sends = pair_sum(keep, swap(send))
    arrived = [along(s, k + 1) for k, s in enumerate(sends)]

    near = (z - jnp.arange(line, dtype=jnp.int32)) % line
    grads = None
    for r in range(PLANE):
        owners = PLANE * near + (p ^ r)
        grads = backward(
            owners, queries, key_rows, values, words_t, lse, context_grads[r], grads
        )

    owned = line_sum(own, arrived, 1.0 / sequences)
    other = swap(owned)
    weight_grad = jnp.where(
        core == 0,
        jnp.concatenate([owned, other], axis=0),
        jnp.concatenate([other, owned], axis=0),
    )
    return (*grads, weight_grad)


def local(queries, key_rows, values, cotangent, out_weight, prob_bits, out_bits):
    tokens, inner_width = queries.shape
    chips, cores = lax.axis_size("fsdp"), lax.axis_size("rep")
    fits = (
        tokens == LENGTH
        and cores == 2
        and chips % PLANE == 0
        and inner_width == chips * 2 * HD
        and out_weight.shape[1] % 1024 == 0
        and prob_bits.shape[2] % 128 == 0
    )
    step = planar if fits else general
    return step(queries, key_rows, values, cotangent, out_weight, prob_bits, out_bits)


def solution(mesh):
    return jax.shard_map(
        local,
        mesh=mesh,
        in_specs=(
            P(("fsdp", "rep"), None),
            P(("fsdp", "rep"), None),
            P(("fsdp", "rep"), None),
            P(("fsdp", "rep"), None),
            P("fsdp", None),
            P(None, ("fsdp", "rep"), None),
            P(None, ("fsdp", "rep"), None),
        ),
        out_specs=(
            P(("fsdp", "rep"), None),
            P(("fsdp", "rep"), None),
            P(("fsdp", "rep"), None),
            P("fsdp", None),
        ),
        check_vma=False,
    )
```
